512 devices in a mesh: dp: 128 (over z, y, core), blk: 4 (over x).
Axes of the slice: x: 4, y: 8, z: 8, core: 2. Of those that a mesh axis runs over, the one named last changes fastest.
Arguments:
- features: bfloat16 [65536, 440], P('dp'), may hold values from -6 to 6
- residual: float32 [65536, 147], P(('dp', 'blk')), may hold values from -6 to 6
- block_weights: float32 [2, 2048, 147], P(None, ('dp', 'blk')), may hold values from -6 to 6
- block_inverse: float32 [2, 2048, 2048], P(None, None, ('dp', 'blk')), as said below
- block_columns: int32 [2, 2048], replicated, may hold values from 0 to 65535, as said below
Outputs:
- residual_out: float32 [65536, 147], P(('dp', 'blk'))
- weights_out: float32 [2, 2048, 147], P(None, ('dp', 'blk'))
The draws below stay inside these ranges and needn't reach their ends.
Inputs may be any that keep to these rules, and one draw needn't show every extreme that they name: `block_columns`: every frame number appears at most once over both blocks. `block_inverse`: each block's matrix is symmetric and positive definite.
All inputs are finite; a program needn't handle non-finite values.
Results may differ from the reference program's by a relative error of at most 0.011.
Values may be sent and summed in bfloat16 or wider, within the bound.
No kernel may reach another device: no remote copies, remote signals or barrier semaphores. Data moves between devices by JAX's collectives and lax.ppermute only.
A program may use at most 64 MiB of HBM per device.

```python
import jax
import jax.numpy as jnp
from jax import lax

D = 440
CLASSES = 147
COLS = 2048
STEPS = 2
ROWS_DEV = 512
ROWS = 65536
N_DP = 128


def draw_block_columns(key, part):
    order = jax.random.permutation(key, ROWS)
    return order[:STEPS * COLS].reshape(STEPS, COLS).astype(jnp.int32)


def draw_block_inverse(key, part):
    key_off = jax.random.fold_in(key, 11)
    key_diag = jax.random.fold_in(key, 12)
    raw = jax.random.normal(key_off, (STEPS, COLS, COLS), jnp.float32) * (0.2 / COLS ** 0.5)
    symmetric = (raw + jnp.swapaxes(raw, 1, 2)) * 2.0 ** (-0.5)
    diagonal = jax.random.uniform(key_diag, (STEPS, COLS), jnp.float32, 0.5, 2.0)
    positions = jnp.arange(COLS)
    identity = (positions[:, None] == positions[None, :]).astype(jnp.float32)
    matrix = symmetric + identity[None, :, :] * diagonal[:, :, None]
    return matrix


def block_levels(own_key, extent, split, least, high):
    loudness, own = 1.0, jax.random.fold_in(own_key, 6)
    for position, parts in split:
        steps = jnp.exp(jax.random.uniform(jax.random.fold_in(own, position), (parts,), jnp.float32, least / len(split), high / len(split)))
        loudness = loudness * jnp.repeat(steps, extent[position] // parts).reshape([-1 if axis == position else 1 for axis in range(len(extent))])
    return loudness


def bell_draw(rng, shape, scale, bound, cuts=(), held_as=jnp.bfloat16):
    loudness = block_levels(rng, shape, cuts, -0.22, 0.18) if cuts else 1.0
    result = jax.random.normal(rng, shape, jnp.float32) * scale * loudness
    return jnp.minimum(jnp.maximum(result, -bound), bound).astype(held_as)


def setup_inputs(seed: int = 0) -> dict:
    streams_of = jax.random.split(jax.random.key(seed), 6)
    return {
        "features": bell_draw(streams_of[0], (ROWS, D), 1.0, 6.0, ((0, 128),)),
        "residual": bell_draw(streams_of[1], (ROWS, CLASSES), 1.0, 6.0, ((0, 512),), jnp.float32),
        "block_weights": bell_draw(streams_of[2], (STEPS, COLS, CLASSES), 1.0, 6.0, ((1, 512),), jnp.float32),
        "block_inverse": draw_block_inverse(jax.random.fold_in(streams_of[5], 71), 0),
        "block_columns": draw_block_columns(jax.random.fold_in(streams_of[5], 71), 0),
    }


RIDGE = 0.3


def kernel_block(frames, centers, center_sq, gamma_rate):
    cross = jnp.dot(frames, centers.T, preferred_element_type=jnp.float32)
    frame_f = frames.astype(jnp.float32)
    frame_sq = jnp.sum(frame_f * frame_f, axis=1)
    return jnp.exp(-gamma_rate * (frame_sq[:, None] + center_sq[None, :] - 2.0 * cross)).astype(jnp.bfloat16)


def reference(features, residual, block_weights, block_inverse, block_columns):
    gamma_rate = 4.0 / D
    feat_blocks = features.reshape(N_DP, ROWS_DEV, D)
    current = residual
    results = []
    for section in range(STEPS):
        columns = block_columns[section]
        centers = jnp.take(features, columns, axis=0)
        center_f = centers.astype(jnp.float32)
        center_sq = jnp.sum(center_f * center_f, axis=1)
        res_blocks = current.reshape(N_DP, ROWS_DEV, CLASSES)

        def grad_part(running, packed):
            frames, res_rows = packed
            kernel = kernel_block(frames, centers, center_sq, gamma_rate)
            term = lax.dot_general(kernel, res_rows.astype(jnp.bfloat16), (((0,), (0,)), ((), ())), preferred_element_type=jnp.float32)
            return running + term, None

        running, _ = lax.scan(grad_part, jnp.zeros((COLS, CLASSES), jnp.float32), (feat_blocks, res_blocks))
        gradient = running - RIDGE * block_weights[section]
        change = jnp.dot(block_inverse[section], gradient, precision=lax.Precision.HIGHEST, preferred_element_type=jnp.float32)
        results.append(block_weights[section] + change)
        change_low = change.astype(jnp.bfloat16)

        def update(packed):
            frames, res_rows = packed
            kernel = kernel_block(frames, centers, center_sq, gamma_rate)
            return res_rows - jnp.dot(kernel, change_low, preferred_element_type=jnp.float32)

        current = lax.map(update, (feat_blocks, res_blocks)).reshape(ROWS, CLASSES)
    return (current, jnp.stack(results))
```

```python
import math

import jax
import jax.numpy as jnp
from jax import lax
from jax.sharding import Mesh
from jax.sharding import PartitionSpec as P

RIDGE = 0.3
DP = ("z", "y", "c")


def swap(pieces, axis):
    return lax.all_to_all(pieces, axis, 0, 0, tiled=True)


def spread(piece, axis):
    return swap(jnp.broadcast_to(piece[None], (lax.axis_size(axis), *piece.shape)), axis)


def total(pieces):
    return jnp.sum(pieces.astype(jnp.float32), axis=0)


def product(left, right, dims, **options):
    return lax.dot_general(
        left, right, (dims, ((), ())), preferred_element_type=jnp.float32, **options
    )


def on_device(features, residual, block_weights, block_inverse, block_columns):
    nz, ny, nc, nx = (lax.axis_size(axis) for axis in ("z", "y", "c", "x"))
    dp, plane = nz * ny * nc, nz * ny
    d, b = lax.axis_index(DP), lax.axis_index("x")
    rows, width = features.shape
    own_rows, classes = residual.shape
    steps, own, _ = block_weights.shape
    columns = block_columns.shape[1]
    group = dp * own
    half = group // nc
    high = -(-classes // 8) * 8
    share = -(-classes // (nz * 8)) * 8
    gamma_rate = 4.0 / width

    inverse_own = (
        block_inverse.reshape(steps, nc, dp // nc, nx, own, own)
        .transpose(0, 5, 1, 3, 2, 4)
        .reshape(steps, own, columns)
    )
    inverse = lax.all_gather(
        inverse_own.astype(jnp.bfloat16).reshape(steps * own, columns), DP, axis=0, tiled=True
    )

    current_own = jnp.pad(residual.T, ((0, high - classes), (0, 0)))
    current = spread(current_own, "x").transpose(1, 0, 2).reshape(high, rows)

    chosen = lax.dynamic_index_in_dim(
        block_columns.reshape(steps, dp, nx, own), b, 2, keepdims=False
    ).reshape(steps * group)
    places = lax.broadcasted_iota(jnp.int32, (steps * group, rows), 1)
    picks = ((chosen - d * rows)[:, None] == places).astype(jnp.bfloat16)
    part = product(picks, features, ((1,), (0,))).astype(jnp.bfloat16)
    part = total(swap(part.reshape(nc, steps * group // nc, width), "c")).astype(jnp.bfloat16)
    part = total(swap(part.reshape(plane, -1, width), ("z", "y"))).astype(jnp.bfloat16)
    part = spread(part, ("z", "y")).reshape(-1, width)
    centers = spread(part, "c").reshape(steps * group, width)

    frame_f = features.astype(jnp.float32)
    frame_sq = jnp.sum(frame_f * frame_f, axis=1)
    center_f = centers.astype(jnp.float32)
    center_sq = jnp.sum(center_f * center_f, axis=1)
    cross = product(centers, features, ((1,), (1,)))
    kernel = jnp.exp(
        -gamma_rate * (frame_sq[None, :] + center_sq[:, None] - 2.0 * cross)
    ).astype(jnp.bfloat16)

    results = []
    for step in range(steps):
        kernel_step = kernel[step * group : (step + 1) * group]
        weights = jnp.pad(block_weights[step].T, ((0, high - classes), (0, 0)))
        gradient = product(current.astype(jnp.bfloat16), kernel_step, ((1,), (1,)))
        lanes = lax.broadcasted_iota(jnp.int32, (high, group), 1) - d * own
        for i in range(own):
            gradient = jnp.where(lanes == i, gradient - RIDGE * weights[:, i : i + 1], gradient)
        gradient = jnp.pad(gradient, ((0, nz * share - high), (0, 0)))
        part = total(swap(gradient.reshape(-1, nc, half).transpose(1, 0, 2), "c"))
        part = total(swap(part.reshape(nz, share, half), "z"))
        part = total(spread(part, "y"))
        part = spread(part.astype(jnp.bfloat16), "z").reshape(nz * share, half)[:high]
        gathered = spread(part, ("c", "x")).transpose(1, 0, 2).reshape(high, columns)
        change_own = product(
            inverse_own[step],
            gathered.astype(jnp.float32),
            ((1,), (1,)),
            precision=lax.Precision.HIGHEST,
        )
        results.append(block_weights[step] + change_own[:, :classes])
        change = product(gathered, inverse, ((1,), (1,))).astype(jnp.bfloat16)
        change = change.reshape(high, dp, steps, own)[:, :, step].reshape(high, group)
        update = product(change, kernel_step, ((1,), (0,))).astype(jnp.bfloat16)
        if step < steps - 1:
            update = total(spread(update, "x"))
            current = current - update
            current_own = current_own - lax.dynamic_slice_in_dim(update, b * own_rows, own_rows, 1)
        else:
            update = update.reshape(high, nx, own_rows).transpose(1, 0, 2)
            current_own = current_own - total(swap(update, "x"))
    return current_own[:classes].T, jnp.stack(results)


def solution(mesh):
    dp, blk = mesh.shape["dp"], mesh.shape["blk"]
    plane = dp // 2
    ny = 1 << (int(math.log2(plane)) // 2)
    fine = Mesh(mesh.devices.reshape(plane // ny, ny, 2, blk), ("z", "y", "c", "x"))
    placed = (
        P(DP, None),
        P((*DP, "x"), None),
        P(None, (*DP, "x"), None),
        P(None, None, (*DP, "x")),
        P(),
    )
    return jax.shard_map(
        on_device,
        mesh=fine,
        in_specs=placed,
        out_specs=(P((*DP, "x"), None), P(None, (*DP, "x"), None)),
        check_vma=False,
    )
```

```python
import math

import jax
import jax.numpy as jnp
from jax import lax
from jax.sharding import Mesh
from jax.sharding import PartitionSpec as P

RIDGE = 0.3
DP = ("z", "y", "c")
PLANE = ("z", "y")
CELL = ("c", "x")


def swap(pieces, axis):
    return lax.all_to_all(pieces, axis, 0, 0, tiled=True)


def spread(piece, axis):
    return swap(jnp.broadcast_to(piece[None], (lax.axis_size(axis), *piece.shape)), axis)


def total(pieces):
    return jnp.sum(pieces.astype(jnp.float32), axis=0)


def side_by_side(pieces):
    count, high, wide = pieces.shape
    return pieces.transpose(1, 0, 2).reshape(high, count * wide)


def product(left, right, dims, **options):
    return lax.dot_general(
        left, right, (dims, ((), ())), preferred_element_type=jnp.float32, **options
    )


def on_device(features, residual, block_weights, block_inverse, block_columns):
    nz, ny, nc, nx = (lax.axis_size(axis) for axis in ("z", "y", "c", "x"))
    plane, cell = nz * ny, nc * nx
    place, member = lax.axis_index(PLANE), lax.axis_index(CELL)
    width = features.shape[1]
    own_rows, classes = residual.shape
    steps, own, _ = block_weights.shape
    columns = block_columns.shape[1]
    group = plane * own
    high = -(-classes // 8) * 8
    share = -(-classes // (nz * 8)) * 8
    gamma_rate = 4.0 / width
    low = jnp.bfloat16

    inverse = (
        block_inverse.astype(low)
        .reshape(steps, plane, cell, own, own)
        .transpose(0, 4, 2, 1, 3)
        .reshape(steps * own, columns)
    )
    inverse = lax.all_gather(inverse, PLANE, axis=0, tiled=True)
    order = lax.broadcasted_iota(jnp.int32, (steps * group, steps * group), 0)
    order = (order // own % plane) * (steps * own) + order // group * own + order % own
    order = order == lax.broadcasted_iota(jnp.int32, order.shape, 1)
    inverse = product(order.astype(low), inverse, ((1,), (0,))).astype(low)

    current = jnp.pad(residual.T, ((0, high - classes), (0, 0)))
    current_low = side_by_side(spread(current.astype(low), CELL))

    frames = spread(features, "c").reshape(-1, width)
    rows = frames.shape[0]
    chosen = lax.dynamic_index_in_dim(
        block_columns.reshape(steps, plane, cell, own), member, 2, keepdims=False
    ).reshape(steps * group)
    spots = lax.broadcasted_iota(jnp.int32, (steps * group, rows), 1)
    picks = ((chosen - place * rows)[:, None] == spots).astype(low)
    part = product(picks, frames, ((1,), (0,))).astype(low)
    part = total(swap(part.reshape(plane, -1, width), PLANE)).astype(low)
    centers = spread(part, PLANE).reshape(steps * group, width)

    frame_f = frames.astype(jnp.float32)
    frame_sq = jnp.sum(frame_f * frame_f, axis=1)
    center_f = centers.astype(jnp.float32)
    center_sq = jnp.sum(center_f * center_f, axis=1)
    cross = product(centers, frames, ((1,), (1,)))
    kernel = jnp.exp(
        -gamma_rate * (frame_sq[None, :] + center_sq[:, None] - 2.0 * cross)
    ).astype(low)

    lanes = lax.broadcasted_iota(jnp.int32, (high, group), 1) - place * own
    results = []
    for step in range(steps):
        block = slice(step * group, (step + 1) * group)
        weights = jnp.pad(block_weights[step].T, ((0, high - classes), (0, 0)))
        gradient = product(current_low, kernel[block], ((1,), (1,)))
        for i in range(own):
            gradient = jnp.where(lanes == i, gradient - RIDGE * weights[:, i : i + 1], gradient)
        gradient = jnp.pad(gradient, ((0, nz * share - high), (0, 0)))
        part = total(swap(gradient.reshape(nz, share, group), "z"))
        part = total(spread(part, "y"))
        part = side_by_side(spread(part.astype(low), CELL))
        part = product(part, inverse[block], ((1,), (1,)))
        change = spread(part, "z").reshape(nz * share, group)[:high]
        update = product(change.astype(low), kernel[block], ((1,), (0,))).astype(low)
        update = update.reshape(high, cell, own_rows).transpose(1, 0, 2)
        current = current - total(swap(update, CELL))
        if step < steps - 1:
            current_low = side_by_side(spread(current.astype(low), CELL))
        change_own = jnp.stack(
            [jnp.sum(jnp.where(lanes == i, change, 0.0), axis=1)[:classes] for i in range(own)]
        )
        results.append(block_weights[step] + change_own)
    return current[:classes].T, jnp.stack(results)


def solution(mesh):
    dp, blk = mesh.shape["dp"], mesh.shape["blk"]
    plane = dp // 2
    ny = 1 << (int(math.log2(plane)) // 2)
    fine = Mesh(mesh.devices.reshape(plane // ny, ny, 2, blk), ("z", "y", "c", "x"))
    placed = (
        P(DP, None),
        P((*DP, "x"), None),
        P(None, (*DP, "x"), None),
        P(None, None, (*DP, "x")),
        P(),
    )
    return jax.shard_map(
        on_device,
        mesh=fine,
        in_specs=placed,
        out_specs=(P((*DP, "x"), None), P(None, (*DP, "x"), None)),
        check_vma=False,
    )
```

```python
import math

import jax
import jax.numpy as jnp
from jax import lax
from jax.sharding import Mesh
from jax.sharding import PartitionSpec as P

RIDGE = 0.3
DP = ("z", "y", "c")
PLANE = ("z", "y")
CELL = ("c", "x")


def swap(pieces, axis):
    return lax.all_to_all(pieces, axis, 0, 0, tiled=True)


def spread(piece, axis):
    return swap(jnp.broadcast_to(piece[None], (lax.axis_size(axis), *piece.shape)), axis)


def total(pieces):
    return jnp.sum(pieces.astype(jnp.float32), axis=0)


def side_by_side(pieces):
    count, high, wide = pieces.shape
    return pieces.transpose(1, 0, 2).reshape(high, count * wide)


def product(left, right, dims, **options):
    return lax.dot_general(
        left, right, (dims, ((), ())), preferred_element_type=jnp.float32, **options
    )


def in_step_order(rows, steps, plane, own):
    count = steps * plane * own
    row = lax.broadcasted_iota(jnp.int32, (count, count), 0)
    source = (row // own % plane) * (steps * own) + row // (plane * own) * own + row % own
    order = source == lax.broadcasted_iota(jnp.int32, (count, count), 1)
    return product(order.astype(rows.dtype), rows, ((1,), (0,))).astype(rows.dtype)


def on_device(features, residual, block_weights, block_inverse, block_columns):
    nz, ny, nc, nx = (lax.axis_size(axis) for axis in ("z", "y", "c", "x"))
    plane, cell = nz * ny, nc * nx
    place, member = lax.axis_index(PLANE), lax.axis_index(CELL)
    width = features.shape[1]
    own_rows, classes = residual.shape
    steps, own, _ = block_weights.shape
    columns = block_columns.shape[1]
    group = plane * own
    high = -(-classes // 8) * 8
    share = -(-classes // (nz * 8)) * 8
    gamma_rate = 4.0 / width
    low = jnp.bfloat16

    span = min(plane, 128 // own)
    row = lax.broadcasted_iota(jnp.int32, (cell * span * own, cell * span * own), 0)
    col = lax.broadcasted_iota(jnp.int32, row.shape, 1)
    there = row // own % cell * (span * own) + row // (own * cell) * own + row % own
    inverse = product(
        block_inverse.transpose(0, 2, 1).astype(low).reshape(steps * own, -1, row.shape[0]),
        (there == col).astype(low),
        ((2,), (0,)),
    ).astype(low)
    inverse = (
        inverse.reshape(steps * own, -1, cell, span * own)
        .transpose(0, 2, 1, 3)
        .reshape(steps * own, columns)
    )
    inverse = lax.all_gather(inverse, PLANE, axis=0, tiled=True)
    current = jnp.pad(residual.T, ((0, high - classes), (0, 0)))
    current_low = side_by_side(lax.all_gather(current.astype(low), CELL))

    other = lax.ppermute(features, "c", [(i, (i + 1) % nc) for i in range(nc)])
    first = lax.axis_index("c") == 0
    frames = jnp.concatenate(
        [jnp.where(first, features, other), jnp.where(first, other, features)]
    )
    rows = frames.shape[0]
    chosen = lax.dynamic_index_in_dim(
        block_columns.reshape(steps, plane, cell, own), member, 2, keepdims=False
    ).reshape(steps * group)
    spots = lax.broadcasted_iota(jnp.int32, (steps * group, rows), 1)
    picks = ((chosen - place * rows)[:, None] == spots).astype(low)
    part = product(picks, frames, ((1,), (0,))).astype(low)
    part = total(swap(part.reshape(plane, -1, width), PLANE)).astype(low)
    centers = spread(part, PLANE).reshape(steps * group, width)

    frame_f = frames.astype(jnp.float32)
    frame_sq = jnp.sum(frame_f * frame_f, axis=1)
    center_f = centers.astype(jnp.float32)
    center_sq = jnp.sum(center_f * center_f, axis=1)
    cross = product(centers, frames, ((1,), (1,)))
    kernel = jnp.exp(
        -gamma_rate * (frame_sq[None, :] + center_sq[:, None] - 2.0 * cross)
    ).astype(low)

    lanes = lax.broadcasted_iota(jnp.int32, (high, group), 1) - place * own
    results = []
    for step in range(steps):
        block = slice(step * group, (step + 1) * group)
        weights = jnp.pad(block_weights[step].T, ((0, high - classes), (0, 0)))
        gradient = product(current_low, kernel[block], ((1,), (1,)))
        for i in range(own):
            gradient = jnp.where(lanes == i, gradient - RIDGE * weights[:, i : i + 1], gradient)
        gradient = jnp.pad(gradient.astype(low), ((0, nz * share - high), (0, 0)))
        part = total(swap(gradient.reshape(nz, share, group), "z"))
        part = total(spread(part.astype(low), "y"))
        part = part.astype(low)
        if step == 0:
            part, inverse = lax.optimization_barrier((part, inverse))
            inverse = in_step_order(inverse, steps, plane, own)
        part = side_by_side(spread(part, CELL))
        part = product(part, inverse[block], ((1,), (1,)))
        change = spread(part, "z").reshape(nz * share, group)[:high]
        update = product(change.astype(low), kernel[block], ((1,), (0,))).astype(low)
        update = update.reshape(high, cell, own_rows).transpose(1, 0, 2)
        current = current - total(swap(update, CELL))
        if step < steps - 1:
            current_low = side_by_side(spread(current.astype(low), CELL))
        change_own = jnp.stack(
            [jnp.sum(jnp.where(lanes == i, change, 0.0), axis=1)[:classes] for i in range(own)]
        )
        results.append(block_weights[step] + change_own)
    return current[:classes].T, jnp.stack(results)


def solution(mesh):
    dp, blk = mesh.shape["dp"], mesh.shape["blk"]
    plane = dp // 2
    ny = 1 << (int(math.log2(plane)) // 2)
    fine = Mesh(mesh.devices.reshape(plane // ny, ny, 2, blk), ("z", "y", "c", "x"))
    placed = (
        P(DP, None),
        P((*DP, "x"), None),
        P(None, (*DP, "x"), None),
        P(None, None, (*DP, "x")),
        P(),
    )
    return jax.shard_map(
        on_device,
        mesh=fine,
        in_specs=placed,
        out_specs=(P((*DP, "x"), None), P(None, (*DP, "x"), None)),
        check_vma=False,
    )
```

```python
import math

import jax
import jax.numpy as jnp
from jax import lax
from jax.sharding import Mesh
from jax.sharding import PartitionSpec as P

RIDGE = 0.3
DP = ("z", "y", "c")
PLANE = ("z", "y")
CELL = ("c", "x")


def swap(pieces, axis):
    return lax.all_to_all(pieces, axis, 0, 0, tiled=True)


def spread(piece, axis):
    return swap(jnp.broadcast_to(piece[None], (lax.axis_size(axis), *piece.shape)), axis)


def both(piece, first):
    other = lax.ppermute(piece, "c", [(0, 1), (1, 0)])
    return jnp.stack([jnp.where(first, piece, other), jnp.where(first, other, piece)])


def total(pieces):
    return jnp.sum(pieces.astype(jnp.float32), axis=0)


def side_by_side(pieces):
    count, high, wide = pieces.shape
    return pieces.transpose(1, 0, 2).reshape(high, count * wide)


def product(left, right, dims, **options):
    return lax.dot_general(
        left, right, (dims, ((), ())), preferred_element_type=jnp.float32, **options
    )


def in_step_order(rows, steps, plane, own):
    count = steps * plane * own
    row = lax.broadcasted_iota(jnp.int32, (count, count), 0)
    source = (row // own % plane) * (steps * own) + row // (plane * own) * own + row % own
    order = source == lax.broadcasted_iota(jnp.int32, (count, count), 1)
    return product(order.astype(rows.dtype), rows, ((1,), (0,))).astype(rows.dtype)


def on_device(features, residual, block_weights, block_inverse, block_columns):
    nz, ny, nc, nx = (lax.axis_size(axis) for axis in ("z", "y", "c", "x"))
    plane, cell = nz * ny, nc * nx
    place, member = lax.axis_index(PLANE), lax.axis_index(CELL)
    width = features.shape[1]
    own_rows, classes = residual.shape
    steps, own, _ = block_weights.shape
    columns = block_columns.shape[1]
    group = plane * own
    high = -(-classes // 8) * 8
    share = -(-classes // (nz * 8)) * 8
    gamma_rate = 4.0 / width
    low = jnp.bfloat16

    span = min(plane, 128 // own)
    row = lax.broadcasted_iota(jnp.int32, (cell * span * own, cell * span * own), 0)
    col = lax.broadcasted_iota(jnp.int32, row.shape, 1)
    there = row // own % cell * (span * own) + row // (own * cell) * own + row % own
    inverse = product(
        block_inverse.transpose(0, 2, 1).astype(low).reshape(steps * own, -1, row.shape[0]),
        (there == col).astype(low),
        ((2,), (0,)),
    ).astype(low)
    inverse = (
        inverse.reshape(steps * own, -1, cell, span * own)
        .transpose(0, 2, 1, 3)
        .reshape(steps * own, columns)
    )
    inverse = lax.all_gather(inverse, PLANE, axis=0, tiled=True)
    current = jnp.pad(residual.T, ((0, high - classes), (0, 0)))
    first = lax.axis_index("c") == 0
    pair = both(current.astype(low), first)
    pair = lax.all_gather(pair, "x")
    current_low = side_by_side(pair.swapaxes(0, 1).reshape(cell, high, own_rows))

    frames = both(features, first).reshape(nc * features.shape[0], width)
    rows = frames.shape[0]
    chosen = lax.dynamic_index_in_dim(
        block_columns.reshape(steps, plane, cell, own), member, 2, keepdims=False
    ).reshape(steps * group)
    spots = lax.broadcasted_iota(jnp.int32, (steps * group, rows), 1)
    picks = ((chosen - place * rows)[:, None] == spots).astype(low)
    part = product(picks, frames, ((1,), (0,))).astype(low)
    part = total(swap(part.reshape(plane, -1, width), PLANE)).astype(low)
    centers = spread(part, PLANE).reshape(steps * group, width)

    frame_f = frames.astype(jnp.float32)
    frame_sq = jnp.sum(frame_f * frame_f, axis=1)
    center_f = centers.astype(jnp.float32)
    center_sq = jnp.sum(center_f * center_f, axis=1)
    cross = product(centers, frames, ((1,), (1,)))
    kernel = jnp.exp(
        -gamma_rate * (frame_sq[None, :] + center_sq[:, None] - 2.0 * cross)
    ).astype(low)

    lanes = lax.broadcasted_iota(jnp.int32, (high, group), 1) - place * own
    results = []
    for step in range(steps):
        block = slice(step * group, (step + 1) * group)
        weights = jnp.pad(block_weights[step].T, ((0, high - classes), (0, 0)))
        gradient = product(current_low, kernel[block], ((1,), (1,)))
        for i in range(own):
            gradient = jnp.where(lanes == i, gradient - RIDGE * weights[:, i : i + 1], gradient)
        gradient = jnp.pad(gradient.astype(low), ((0, nz * share - high), (0, 0)))
        part = total(swap(gradient.reshape(nz, share, group), "z"))
        part = total(spread(part.astype(low), "y"))
        part = part.astype(low)
        if step == 0:
            part, inverse = lax.optimization_barrier((part, inverse))
            inverse = in_step_order(inverse, steps, plane, own)
        part = side_by_side(spread(part, CELL))
        part = product(part, inverse[block], ((1,), (1,))).astype(low)
        change = spread(part, "z").reshape(nz * share, group)[:high]
        update = product(change, kernel[block], ((1,), (0,))).astype(low)
        update = update.reshape(high, cell, own_rows).transpose(1, 0, 2)
        current = current - total(swap(update, CELL))
        if step < steps - 1:
            current_low = side_by_side(spread(current.astype(low), CELL))
        change_own = jnp.stack(
            [jnp.sum(jnp.where(lanes == i, change, 0.0), axis=1)[:classes] for i in range(own)]
        )
        results.append(block_weights[step] + change_own)
    return current[:classes].T, jnp.stack(results)


def solution(mesh):
    dp, blk = mesh.shape["dp"], mesh.shape["blk"]
    plane = dp // 2
    ny = 1 << (int(math.log2(plane)) // 2)
    fine = Mesh(mesh.devices.reshape(plane // ny, ny, 2, blk), ("z", "y", "c", "x"))
    placed = (
        P(DP, None),
        P((*DP, "x"), None),
        P(None, (*DP, "x"), None),
        P(None, None, (*DP, "x")),
        P(),
    )
    return jax.shard_map(
        on_device,
        mesh=fine,
        in_specs=placed,
        out_specs=(P((*DP, "x"), None), P(None, (*DP, "x"), None)),
        check_vma=False,
    )
```

```python
import math

import jax
import jax.numpy as jnp
from jax import lax
from jax.experimental import pallas as pl
from jax.experimental.pallas import tpu as pltpu
from jax.sharding import Mesh
from jax.sharding import PartitionSpec as P

RIDGE = 0.3
DP = ("z", "y", "c")
PLANE = ("z", "y")
CELL = ("c", "x")


def swap(pieces, axis):
    return lax.all_to_all(pieces, axis, 0, 0, tiled=True)


def spread(piece, axis):
    return swap(jnp.broadcast_to(piece[None], (lax.axis_size(axis), *piece.shape)), axis)


def both(piece, first):
    other = lax.ppermute(piece, "c", [(0, 1), (1, 0)])
    return jnp.stack([jnp.where(first, piece, other), jnp.where(first, other, piece)])


def total(pieces):
    return jnp.sum(pieces.astype(jnp.float32), axis=0)


def side_by_side(pieces):
    count, high, wide = pieces.shape
    return pieces.transpose(1, 0, 2).reshape(high, count * wide)


def product(left, right, dims, **options):
    return lax.dot_general(
        left, right, (dims, ((), ())), preferred_element_type=jnp.float32, **options
    )


def arranged(rows, plane, cell):
    steps, own, columns = rows.shape
    count = steps * own
    if columns % 2048 or count != 8 or cell * own != 32:
        rows = rows.astype(jnp.bfloat16).reshape(count, plane, cell, own)
        return rows.transpose(0, 2, 1, 3).reshape(count, columns)
    blocks = columns // 128
    run = 128 // cell

    def kernel(rows_ref, out_ref):
        tall = jnp.concatenate([rows_ref[step] for step in range(steps)], axis=0)
        tall = jnp.concatenate([tall[:, 128 * q : 128 * (q + 1)] for q in range(blocks)], axis=0)
        source = lax.broadcasted_iota(jnp.int32, (128, 128), 0)
        target = lax.broadcasted_iota(jnp.int32, (128, 128), 1)
        member, lane = (source >> 2) & 7, ((source >> 5) << 2) | (source & 3)
        order = jnp.where(member * run + lane == target, 1.0, 0.0).astype(jnp.bfloat16)
        tall = jnp.dot(tall.astype(jnp.bfloat16), order, preferred_element_type=jnp.float32)
        part = lax.broadcasted_iota(jnp.int32, (count, 128), 1) >> 4
        for out in range(blocks):
            member, first = out * cell // blocks, out % (blocks // cell) * cell
            joined = jnp.zeros((count, 128), jnp.float32)
            for k in range(cell):
                q = first + k
                piece = tall[count * q : count * (q + 1)]
                if k != member:
                    piece = pltpu.roll(piece, (k - member) * run % 128, 1)
                joined = jnp.where(part == k, piece, joined)
            out_ref[:, 128 * out : 128 * (out + 1)] = joined.astype(out_ref.dtype)

    return pl.pallas_call(
        kernel,
        out_shape=jax.ShapeDtypeStruct((count, columns), jnp.bfloat16),
        name="arrange",
    )(rows)


def step_places(step, steps, plane, own):
    shape = (plane * own, steps * plane * own)
    row = lax.broadcasted_iota(jnp.int32, shape, 0)
    source = row // own * (steps * own) + step * own + row % own
    return (source == lax.broadcasted_iota(jnp.int32, shape, 1)).astype(jnp.bfloat16)


def on_device(features, residual, block_weights, block_inverse, block_columns):
    nz, ny, nc, nx = (lax.axis_size(axis) for axis in ("z", "y", "c", "x"))
    plane, cell = nz * ny, nc * nx
    place, member = lax.axis_index(PLANE), lax.axis_index(CELL)
    width = features.shape[1]
    own_rows, classes = residual.shape
    steps, own, _ = block_weights.shape
    columns = block_columns.shape[1]
    group = plane * own
    high = -(-classes // 8) * 8
    share = -(-classes // (nz * 8)) * 8
    tall = nz * share
    gamma_rate = 4.0 / width
    low = jnp.bfloat16

    inverse = arranged(block_inverse.transpose(0, 2, 1), plane, cell)
    inverse = lax.all_gather(inverse, PLANE, axis=0, tiled=True)
    current = jnp.pad(residual.T, ((0, high - classes), (0, 0)))
    first = lax.axis_index("c") == 0
    pair = both(current.astype(low), first)
    pair = lax.all_gather(pair, "x")
    current_low = side_by_side(pair.swapaxes(0, 1).reshape(cell, high, own_rows))

    frames = both(features, first).reshape(nc * features.shape[0], width)
    rows = frames.shape[0]
    chosen = lax.dynamic_index_in_dim(
        block_columns.reshape(steps, plane, cell, own), member, 2, keepdims=False
    ).reshape(steps * group)
    spots = lax.broadcasted_iota(jnp.int32, (steps * group, rows), 1)
    picks = ((chosen - place * rows)[:, None] == spots).astype(low)
    part = product(picks, frames, ((1,), (0,))).astype(low)
    part = total(swap(part.reshape(plane, -1, width), PLANE)).astype(low)
    centers = spread(part, PLANE).reshape(steps * group, width)

    frame_f = frames.astype(jnp.float32)
    frame_sq = jnp.sum(frame_f * frame_f, axis=1)
    center_f = centers.astype(jnp.float32)
    center_sq = jnp.sum(center_f * center_f, axis=1)
    cross = product(centers, frames, ((1,), (1,)))
    kernel = jnp.exp(
        -gamma_rate * (frame_sq[None, :] + center_sq[:, None] - 2.0 * cross)
    ).astype(low)

    lanes = lax.broadcasted_iota(jnp.int32, (tall, group), 1) - place * own
    results = []
    for step in range(steps):
        block = slice(step * group, (step + 1) * group)
        weights = jnp.pad(block_weights[step].T, ((0, tall - classes), (0, 0)))
        current_low = jnp.pad(current_low, ((0, tall - high), (0, 0)))
        gradient = product(current_low, kernel[block], ((1,), (1,)))
        for i in range(own):
            gradient = jnp.where(lanes == i, gradient - RIDGE * weights[:, i : i + 1], gradient)
        gradient = gradient.astype(low)
        part = total(swap(gradient.reshape(nz, share, group), "z"))
        part = total(spread(part.astype(low), "y"))
        part = part.astype(low)
        places = step_places(step, steps, plane, own)
        if step == 0:
            part = side_by_side(spread(part, CELL))
            part = product(part, inverse, ((1,), (1,))).astype(low)
            part = product(part, places, ((1,), (1,))).astype(low)
        else:
            part, inverse = lax.optimization_barrier((part, inverse))
            inverse_step = product(places, inverse, ((1,), (0,))).astype(low)
            part = side_by_side(spread(part, CELL))
            part = product(part, inverse_step, ((1,), (1,))).astype(low)
        change = spread(part, "z").reshape(tall, group)[:high]
        update = product(change, kernel[block], ((1,), (0,))).astype(low)
        update = update.reshape(high, cell, own_rows).transpose(1, 0, 2)
        current = current - total(swap(update, CELL))
        if step < steps - 1:
            current_low = side_by_side(spread(current.astype(low), CELL))
        change_own = jnp.stack(
            [jnp.sum(jnp.where(lanes[:high] == i, change, 0.0), axis=1)[:classes] for i in range(own)]
        )
        results.append(block_weights[step] + change_own)
    return current[:classes].T, jnp.stack(results)


def solution(mesh):
    dp, blk = mesh.shape["dp"], mesh.shape["blk"]
    plane = dp // 2
    ny = 1 << (int(math.log2(plane)) // 2)
    fine = Mesh(mesh.devices.reshape(plane // ny, ny, 2, blk), ("z", "y", "c", "x"))
    placed = (
        P(DP, None),
        P((*DP, "x"), None),
        P(None, (*DP, "x"), None),
        P(None, None, (*DP, "x")),
        P(),
    )
    return jax.shard_map(
        on_device,
        mesh=fine,
        in_specs=placed,
        out_specs=(P((*DP, "x"), None), P(None, (*DP, "x"), None)),
        check_vma=False,
    )
```

```python
import math

import jax
import jax.numpy as jnp
from jax import lax
from jax.experimental import pallas as pl
from jax.experimental.pallas import tpu as pltpu
from jax.sharding import Mesh
from jax.sharding import PartitionSpec as P

RIDGE = 0.3
DP = ("z", "y", "c")
PLANE = ("z", "y")
CELL = ("c", "x")


def swap(pieces, axis):
    return lax.all_to_all(pieces, axis, 0, 0, tiled=True)


def spread(piece, axis):
    return swap(jnp.broadcast_to(piece[None], (lax.axis_size(axis), *piece.shape)), axis)


def ordered(piece, other, first):
    return jnp.stack([jnp.where(first, piece, other), jnp.where(first, other, piece)])


def total(pieces):
    return jnp.sum(pieces.astype(jnp.float32), axis=0)


def side_by_side(pieces):
    count, high, wide = pieces.shape
    return pieces.transpose(1, 0, 2).reshape(high, count * wide)


def product(left, right, dims, **options):
    return lax.dot_general(
        left, right, (dims, ((), ())), preferred_element_type=jnp.float32, **options
    )


def arranged(rows, numbers, plane, cell):
    steps, own, columns = rows.shape
    count, group = steps * own, plane * own
    if columns % 2048 or count != 8 or cell * own != 32:
        rows = rows.astype(jnp.bfloat16).reshape(count, plane, cell, own)
        numbers = numbers.reshape(steps, plane, cell, own).transpose(2, 0, 1, 3)
        return (
            rows.transpose(0, 2, 1, 3).reshape(count, columns),
            numbers.reshape(cell, steps, group),
        )
    blocks = columns // 128
    run = 128 // cell

    def kernel(rows_ref, numbers_ref, rows_out, numbers_out):
        number = numbers_ref[...]
        tall = [rows_ref[step] for step in range(steps)]
        tall += [(number >> 8).astype(jnp.float32), (number & 255).astype(jnp.float32)]
        tall += [jnp.zeros((16 - count - 2 * steps, columns), jnp.float32)]
        tall = jnp.concatenate(tall, axis=0)
        tall = jnp.concatenate([tall[:, 128 * q : 128 * (q + 1)] for q in range(blocks)], axis=0)
        source = lax.broadcasted_iota(jnp.int32, (128, 128), 0)
        target = lax.broadcasted_iota(jnp.int32, (128, 128), 1)
        member, lane = (source >> 2) & 7, ((source >> 5) << 2) | (source & 3)
        order = jnp.where(member * run + lane == target, 1.0, 0.0).astype(jnp.bfloat16)
        tall = jnp.dot(tall.astype(jnp.bfloat16), order, preferred_element_type=jnp.float32)
        part = lax.broadcasted_iota(jnp.int32, (16, 128), 1) >> 4
        wide = blocks // cell
        for out in range(blocks):
            member, first = out // wide, out % wide * cell
            joined = jnp.zeros((16, 128), jnp.float32)
            for k in range(cell):
                q = first + k
                piece = tall[16 * q : 16 * (q + 1)]
                if k != member:
                    piece = pltpu.roll(piece, (k - member) * run % 128, 1)
                joined = jnp.where(part == k, piece, joined)
            rows_out[:, 128 * out : 128 * (out + 1)] = joined[:count].astype(rows_out.dtype)
            number = joined[count : count + steps] * 256.0 + joined[count + steps : count + 2 * steps]
            at = out % wide * 128
            numbers_out[member, :, at : at + 128] = number.astype(jnp.int32)

    return pl.pallas_call(
        kernel,
        out_shape=(
            jax.ShapeDtypeStruct((count, columns), jnp.bfloat16),
            jax.ShapeDtypeStruct((cell, steps, group), jnp.int32),
        ),
        name="arrange",
    )(rows, numbers)


def step_places(step, steps, plane, own):
    shape = (plane * own, steps * plane * own)
    row = lax.broadcasted_iota(jnp.int32, shape, 0)
    source = row // own * (steps * own) + step * own + row % own
    return (source == lax.broadcasted_iota(jnp.int32, shape, 1)).astype(jnp.bfloat16)


def on_device(features, residual, block_weights, block_inverse, block_columns):
    nz, ny, nc, nx = (lax.axis_size(axis) for axis in ("z", "y", "c", "x"))
    plane, cell = nz * ny, nc * nx
    place, member = lax.axis_index(PLANE), lax.axis_index(CELL)
    width = features.shape[1]
    own_rows, classes = residual.shape
    steps, own, _ = block_weights.shape
    columns = block_columns.shape[1]
    group = plane * own
    high = -(-classes // 8) * 8
    share = -(-classes // (nz * 8)) * 8
    tall = nz * share
    gamma_rate = 4.0 / width
    low = jnp.bfloat16

    inverse, chosen = arranged(block_inverse.transpose(0, 2, 1), block_columns, plane, cell)
    inverse = lax.all_gather(inverse, PLANE, axis=0, tiled=True)
    current = jnp.pad(residual.T, ((0, high - classes), (0, 0)))
    first = lax.axis_index("c") == 0

    chosen = lax.dynamic_index_in_dim(chosen, member, 0, keepdims=False).reshape(steps * group)

    other = lax.ppermute(features, "c", [(0, 1), (1, 0)])
    frames = ordered(features, other, first).reshape(nc * features.shape[0], width)
    spots = lax.broadcasted_iota(jnp.int32, (steps * group, frames.shape[0]), 1)
    picks = ((chosen - place * frames.shape[0])[:, None] == spots).astype(low)
    part = product(picks, frames, ((1,), (0,))).astype(low)
    part, pair = lax.optimization_barrier((part, residual))
    pair = jnp.pad(pair.T, ((0, high - classes), (0, 0))).astype(low)
    pair = ordered(pair, lax.ppermute(pair, "c", [(0, 1), (1, 0)]), first)
    part = total(swap(part.reshape(plane, -1, width), PLANE)).astype(low)
    places = step_places(0, steps, plane, own)
    part, pair, places = lax.optimization_barrier((part, pair, places))
    pair = lax.all_gather(pair, "x")
    current_low = side_by_side(pair.swapaxes(0, 1).reshape(cell, high, own_rows))
    centers = spread(part, PLANE).reshape(steps * group, width)

    frame_f = frames.astype(jnp.float32)
    frame_sq = jnp.sum(frame_f * frame_f, axis=1)
    center_f = centers.astype(jnp.float32)
    center_sq = jnp.sum(center_f * center_f, axis=1)
    cross = product(centers, frames, ((1,), (1,)))
    kernel = jnp.exp(
        -gamma_rate * (frame_sq[None, :] + center_sq[:, None] - 2.0 * cross)
    ).astype(low)

    lanes = lax.broadcasted_iota(jnp.int32, (tall, group), 1) - place * own
    results = []
    for step in range(steps):
        block = slice(step * group, (step + 1) * group)
        weights = jnp.pad(block_weights[step].T, ((0, tall - classes), (0, 0)))
        current_low = jnp.pad(current_low, ((0, tall - high), (0, 0)))
        gradient = product(current_low, kernel[block], ((1,), (1,)))
        for i in range(own):
            gradient = jnp.where(lanes == i, gradient - RIDGE * weights[:, i : i + 1], gradient)
        gradient = gradient.astype(low)
        part = total(swap(gradient.reshape(nz, share, group), "z"))
        part = total(spread(part.astype(low), "y"))
        part = part.astype(low)
        if step > 0:
            places = step_places(step, steps, plane, own)
        part = side_by_side(spread(part, CELL))
        part = product(part, inverse, ((1,), (1,))).astype(low)
        part = product(part, places, ((1,), (1,))).astype(low)
        change = spread(part, "z").reshape(tall, group)[:high]
        update = product(change, kernel[block], ((1,), (0,))).astype(low)
        update = update.reshape(high, cell, own_rows).transpose(1, 0, 2)
        current = current - total(swap(update, CELL))
        if step < steps - 1:
            current_low = side_by_side(spread(current.astype(low), CELL))
        change_own = jnp.stack(
            [jnp.sum(jnp.where(lanes[:high] == i, change, 0.0), axis=1)[:classes] for i in range(own)]
        )
        results.append(block_weights[step] + change_own)
    return current[:classes].T, jnp.stack(results)


def solution(mesh):
    dp, blk = mesh.shape["dp"], mesh.shape["blk"]
    plane = dp // 2
    ny = 1 << (int(math.log2(plane)) // 2)
    fine = Mesh(mesh.devices.reshape(plane // ny, ny, 2, blk), ("z", "y", "c", "x"))
    placed = (
        P(DP, None),
        P((*DP, "x"), None),
        P(None, (*DP, "x"), None),
        P(None, None, (*DP, "x")),
        P(),
    )
    return jax.shard_map(
        on_device,
        mesh=fine,
        in_specs=placed,
        out_specs=(P((*DP, "x"), None), P(None, (*DP, "x"), None)),
        check_vma=False,
    )
```

```python
import math

import jax
import jax.numpy as jnp
from jax import lax
from jax.experimental import pallas as pl
from jax.experimental.pallas import tpu as pltpu
from jax.sharding import Mesh
from jax.sharding import PartitionSpec as P

RIDGE = 0.3
DP = ("z", "y", "c")
PLANE = ("z", "y")
CELL = ("c", "x")


def swap(pieces, axis):
    return lax.all_to_all(pieces, axis, 0, 0, tiled=True)


def spread(piece, axis):
    return swap(jnp.broadcast_to(piece[None], (lax.axis_size(axis), *piece.shape)), axis)


def ordered(piece, other, first):
    return jnp.stack([jnp.where(first, piece, other), jnp.where(first, other, piece)])


def total(pieces):
    return jnp.sum(pieces.astype(jnp.float32), axis=0)


def side_by_side(pieces):
    count, high, wide = pieces.shape
    return pieces.transpose(1, 0, 2).reshape(high, count * wide)


def product(left, right, dims, **options):
    return lax.dot_general(
        left, right, (dims, ((), ())), preferred_element_type=jnp.float32, **options
    )


def arranged(rows, numbers, plane, cell):
    steps, own, columns = rows.shape
    count, group = steps * own, plane * own
    if columns % 2048 or count != 8 or cell * own != 32:
        rows = rows.astype(jnp.bfloat16).reshape(count, plane, cell, own)
        numbers = numbers.reshape(steps, plane, cell, own).transpose(2, 0, 1, 3)
        return (
            rows.transpose(0, 2, 1, 3).reshape(count, columns),
            numbers.reshape(cell, steps, group),
        )
    blocks = columns // 128
    run = 128 // cell

    def kernel(rows_ref, numbers_ref, rows_out, numbers_out):
        number = numbers_ref[...]
        tall = [rows_ref[step] for step in range(steps)]
        tall += [(number >> 8).astype(jnp.float32), (number & 255).astype(jnp.float32)]
        tall += [jnp.zeros((16 - count - 2 * steps, columns), jnp.float32)]
        tall = jnp.concatenate(tall, axis=0)
        tall = jnp.concatenate([tall[:, 128 * q : 128 * (q + 1)] for q in range(blocks)], axis=0)
        source = lax.broadcasted_iota(jnp.int32, (128, 128), 0)
        target = lax.broadcasted_iota(jnp.int32, (128, 128), 1)
        member, lane = (source >> 2) & 7, ((source >> 5) << 2) | (source & 3)
        order = jnp.where(member * run + lane == target, 1.0, 0.0).astype(jnp.bfloat16)
        tall = jnp.dot(tall.astype(jnp.bfloat16), order, preferred_element_type=jnp.float32)
        part = lax.broadcasted_iota(jnp.int32, (16, 128), 1) >> 4
        wide = blocks // cell
        for out in range(blocks):
            member, first = out // wide, out % wide * cell
            joined = jnp.zeros((16, 128), jnp.float32)
            for k in range(cell):
                q = first + k
                piece = tall[16 * q : 16 * (q + 1)]
                if k != member:
                    piece = pltpu.roll(piece, (k - member) * run % 128, 1)
                joined = jnp.where(part == k, piece, joined)
            rows_out[:, 128 * out : 128 * (out + 1)] = joined[:count].astype(rows_out.dtype)
            number = joined[count : count + steps] * 256.0 + joined[count + steps : count + 2 * steps]
            at = out % wide * 128
            numbers_out[member, :, at : at + 128] = number.astype(jnp.int32)

    return pl.pallas_call(
        kernel,
        out_shape=(
            jax.ShapeDtypeStruct((count, columns), jnp.bfloat16),
            jax.ShapeDtypeStruct((cell, steps, group), jnp.int32),
        ),
        name="arrange",
    )(rows, numbers)


def step_places(step, steps, plane, own):
    shape = (plane * own, steps * plane * own)
    row = lax.broadcasted_iota(jnp.int32, shape, 0)
    source = row // own * (steps * own) + step * own + row % own
    return (source == lax.broadcasted_iota(jnp.int32, shape, 1)).astype(jnp.bfloat16)


def on_device(features, residual, block_weights, block_inverse, block_columns):
    nz, ny, nc, nx = (lax.axis_size(axis) for axis in ("z", "y", "c", "x"))
    plane, cell = nz * ny, nc * nx
    place, member = lax.axis_index(PLANE), lax.axis_index(CELL)
    width = features.shape[1]
    own_rows, classes = residual.shape
    steps, own, _ = block_weights.shape
    columns = block_columns.shape[1]
    group = plane * own
    high = -(-classes // 8) * 8
    share = -(-classes // (nz * 8)) * 8
    tall = nz * share
    gamma_rate = 4.0 / width
    low = jnp.bfloat16

    inverse, chosen = arranged(block_inverse.transpose(0, 2, 1), block_columns, plane, cell)
    inverse = lax.all_gather(inverse, PLANE, axis=0, tiled=True)
    current = jnp.pad(residual.T, ((0, high - classes), (0, 0)))
    first = lax.axis_index("c") == 0

    chosen = lax.dynamic_index_in_dim(chosen, member, 0, keepdims=False).reshape(steps * group)

    def picked(block, holder):
        spots = lax.broadcasted_iota(jnp.int32, (steps * group, block.shape[0]), 1)
        picks = ((chosen - holder * block.shape[0])[:, None] == spots).astype(low)
        return product(picks, block, ((1,), (0,)))

    core = lax.axis_index("c")
    other = lax.ppermute(features, "c", [(0, 1), (1, 0)])
    frames = ordered(features, other, first).reshape(nc * features.shape[0], width)
    part = picked(features, place * nc + core) + picked(other, place * nc + 1 - core)
    part = part.astype(low)
    part, pair = lax.optimization_barrier((part, residual))
    pair = jnp.pad(pair.T, ((0, high - classes), (0, 0))).astype(low)
    pair = ordered(pair, lax.ppermute(pair, "c", [(0, 1), (1, 0)]), first)
    part = total(swap(part.reshape(plane, -1, width), PLANE)).astype(low)
    places = step_places(0, steps, plane, own)
    part, pair, places = lax.optimization_barrier((part, pair, places))
    pair = lax.all_gather(pair, "x")
    current_low = side_by_side(pair.swapaxes(0, 1).reshape(cell, high, own_rows))
    centers = spread(part, PLANE).reshape(steps * group, width)

    frame_f = frames.astype(jnp.float32)
    frame_sq = jnp.sum(frame_f * frame_f, axis=1)
    center_f = centers.astype(jnp.float32)
    center_sq = jnp.sum(center_f * center_f, axis=1)
    cross = product(centers, frames, ((1,), (1,)))
    kernel = jnp.exp(
        -gamma_rate * (frame_sq[None, :] + center_sq[:, None] - 2.0 * cross)
    ).astype(low)

    lanes = lax.broadcasted_iota(jnp.int32, (tall, group), 1) - place * own
    results = []
    for step in range(steps):
        block = slice(step * group, (step + 1) * group)
        weights = jnp.pad(block_weights[step].T, ((0, tall - classes), (0, 0)))
        current_low = jnp.pad(current_low, ((0, tall - high), (0, 0)))
        gradient = product(current_low, kernel[block], ((1,), (1,)))
        for i in range(own):
            gradient = jnp.where(lanes == i, gradient - RIDGE * weights[:, i : i + 1], gradient)
        gradient = gradient.astype(low)
        part = total(swap(gradient.reshape(nz, share, group), "z"))
        part = total(spread(part.astype(low), "y"))
        part = part.astype(low)
        if step > 0:
            places = step_places(step, steps, plane, own)
        part = side_by_side(spread(part, CELL))
        part = product(part, inverse, ((1,), (1,))).astype(low)
        part = product(part, places, ((1,), (1,))).astype(low)
        change = spread(part, "z").reshape(tall, group)[:high]
        update = product(change, kernel[block], ((1,), (0,))).astype(low)
        update = update.reshape(high, cell, own_rows).transpose(1, 0, 2)
        current = current - total(swap(update, CELL))
        if step < steps - 1:
            current_low = side_by_side(spread(current.astype(low), CELL))
        change_own = jnp.stack(
            [jnp.sum(jnp.where(lanes[:high] == i, change, 0.0), axis=1)[:classes] for i in range(own)]
        )
        results.append(block_weights[step] + change_own)
    return current[:classes].T, jnp.stack(results)


def solution(mesh):
    dp, blk = mesh.shape["dp"], mesh.shape["blk"]
    plane = dp // 2
    ny = 1 << (int(math.log2(plane)) // 2)
    fine = Mesh(mesh.devices.reshape(plane // ny, ny, 2, blk), ("z", "y", "c", "x"))
    placed = (
        P(DP, None),
        P((*DP, "x"), None),
        P(None, (*DP, "x"), None),
        P(None, None, (*DP, "x")),
        P(),
    )
    return jax.shard_map(
        on_device,
        mesh=fine,
        in_specs=placed,
        out_specs=(P((*DP, "x"), None), P(None, (*DP, "x"), None)),
        check_vma=False,
    )
```

```python
import math

import jax
import jax.numpy as jnp
from jax import lax
from jax.experimental import pallas as pl
from jax.experimental.pallas import tpu as pltpu
from jax.sharding import Mesh
from jax.sharding import PartitionSpec as P

RIDGE = 0.3
DP = ("z", "y", "c")
PLANE = ("z", "y")
CELL = ("c", "x")


def swap(pieces, axis):
    return lax.all_to_all(pieces, axis, 0, 0, tiled=True)


def spread(piece, axis):
    return swap(jnp.broadcast_to(piece[None], (lax.axis_size(axis), *piece.shape)), axis)


def ordered(piece, other, first):
    return jnp.stack([jnp.where(first, piece, other), jnp.where(first, other, piece)])


def total(pieces):
    return jnp.sum(pieces.astype(jnp.float32), axis=0)


def side_by_side(pieces):
    count, high, wide = pieces.shape
    return pieces.transpose(1, 0, 2).reshape(high, count * wide)


def product(left, right, dims, **options):
    return lax.dot_general(
        left, right, (dims, ((), ())), preferred_element_type=jnp.float32, **options
    )


def arranged(rows, numbers, plane, cell, where):
    steps, own, columns = rows.shape
    count, group = steps * own, plane * own
    if columns % 2048 or count != 8 or cell * own != 32:
        rows = rows.astype(jnp.bfloat16).reshape(count, plane, cell, own)
        member, base = where()
        numbers = numbers.reshape(steps, plane, cell, own).transpose(2, 0, 1, 3)
        numbers = lax.dynamic_index_in_dim(numbers, member, 0, keepdims=False)
        return (
            rows.transpose(0, 2, 1, 3).reshape(count, columns),
            numbers.reshape(steps, group) - base,
        )
    blocks = columns // 128
    run = 128 // cell

    def kernel(rows_ref, numbers_ref, rows_out, numbers_out):
        number = numbers_ref[...]
        tall = [rows_ref[step] for step in range(steps)]
        tall += [(number >> 8).astype(jnp.float32), (number & 255).astype(jnp.float32)]
        tall += [jnp.zeros((16 - count - 2 * steps, columns), jnp.float32)]
        tall = jnp.concatenate(tall, axis=0)
        tall = jnp.concatenate([tall[:, 128 * q : 128 * (q + 1)] for q in range(blocks)], axis=0)
        source = lax.broadcasted_iota(jnp.int32, (128, 128), 0)
        target = lax.broadcasted_iota(jnp.int32, (128, 128), 1)
        member, lane = (source >> 2) & 7, ((source >> 5) << 2) | (source & 3)
        order = jnp.where(member * run + lane == target, 1.0, 0.0).astype(jnp.bfloat16)
        tall = jnp.dot(tall.astype(jnp.bfloat16), order, preferred_element_type=jnp.float32)
        part = lax.broadcasted_iota(jnp.int32, (16, 128), 1) >> 4
        wide = blocks // cell
        here, base = where()
        found = [jnp.zeros((steps, 128), jnp.float32)] * wide
        for out in range(blocks):
            member, first = out // wide, out % wide * cell
            joined = jnp.zeros((16, 128), jnp.float32)
            for k in range(cell):
                q = first + k
                piece = tall[16 * q : 16 * (q + 1)]
                if k != member:
                    piece = pltpu.roll(piece, (k - member) * run % 128, 1)
                joined = jnp.where(part == k, piece, joined)
            rows_out[:, 128 * out : 128 * (out + 1)] = joined[:count].astype(rows_out.dtype)
            number = joined[count : count + steps] * 256.0 + joined[count + steps : count + 2 * steps]
            at = out % wide
            found[at] = jnp.where(here == member, number, found[at])
        for at in range(wide):
            local = found[at].astype(jnp.int32) - base
            numbers_out[:, 128 * at : 128 * (at + 1)] = local

    return pl.pallas_call(
        kernel,
        out_shape=(
            jax.ShapeDtypeStruct((count, columns), jnp.bfloat16),
            jax.ShapeDtypeStruct((steps, group), jnp.int32),
        ),
        name="arrange",
    )(rows, numbers)


def step_places(step, steps, plane, own):
    shape = (plane * own, steps * plane * own)
    row = lax.broadcasted_iota(jnp.int32, shape, 0)
    source = row // own * (steps * own) + step * own + row % own
    return (source == lax.broadcasted_iota(jnp.int32, shape, 1)).astype(jnp.bfloat16)


def on_device(features, residual, block_weights, block_inverse, block_columns):
    nz, ny, nc, nx = (lax.axis_size(axis) for axis in ("z", "y", "c", "x"))
    plane, cell = nz * ny, nc * nx
    place, member = lax.axis_index(PLANE), lax.axis_index(CELL)
    width = features.shape[1]
    own_rows, classes = residual.shape
    steps, own, _ = block_weights.shape
    columns = block_columns.shape[1]
    group = plane * own
    high = -(-classes // 8) * 8
    share = -(-classes // (nz * 8)) * 8
    tall = nz * share
    gamma_rate = 4.0 / width
    low = jnp.bfloat16

    def where():
        at = lax.axis_index("z") * ny + lax.axis_index("y")
        return lax.axis_index("c") * nx + lax.axis_index("x"), at * nc * features.shape[0]

    inverse, chosen = arranged(block_inverse.transpose(0, 2, 1), block_columns, plane, cell, where)
    inverse = lax.all_gather(inverse, PLANE, axis=0, tiled=True)
    current = jnp.pad(residual.T, ((0, high - classes), (0, 0)))
    first = lax.axis_index("c") == 0

    chosen = chosen.reshape(steps * group)
    other = lax.ppermute(features, "c", [(0, 1), (1, 0)])
    frames = ordered(features, other, first).reshape(nc * features.shape[0], width)
    spots = lax.broadcasted_iota(jnp.int32, (steps * group, frames.shape[0]), 1)
    picks = (chosen[:, None] == spots).astype(low)
    part = product(picks, frames, ((1,), (0,))).astype(low)
    part, pair = lax.optimization_barrier((part, residual))
    pair = jnp.pad(pair.T, ((0, high - classes), (0, 0))).astype(low)
    pair = ordered(pair, lax.ppermute(pair, "c", [(0, 1), (1, 0)]), first)
    part = total(swap(part.reshape(plane, -1, width), PLANE)).astype(low)
    places = step_places(0, steps, plane, own)
    part, pair, places = lax.optimization_barrier((part, pair, places))
    pair = lax.all_gather(pair, "x")
    current_low = side_by_side(pair.swapaxes(0, 1).reshape(cell, high, own_rows))
    centers = spread(part, PLANE).reshape(steps * group, width)

    frame_f = frames.astype(jnp.float32)
    frame_sq = jnp.sum(frame_f * frame_f, axis=1)
    center_f = centers.astype(jnp.float32)
    center_sq = jnp.sum(center_f * center_f, axis=1)
    cross = product(centers, frames, ((1,), (1,)))
    kernel = jnp.exp(
        -gamma_rate * (frame_sq[None, :] + center_sq[:, None] - 2.0 * cross)
    ).astype(low)

    lanes = lax.broadcasted_iota(jnp.int32, (tall, group), 1) - place * own
    results = []
    for step in range(steps):
        block = slice(step * group, (step + 1) * group)
        weights = jnp.pad(block_weights[step].T, ((0, tall - classes), (0, 0)))
        current_low = jnp.pad(current_low, ((0, tall - high), (0, 0)))
        gradient = product(current_low, kernel[block], ((1,), (1,)))
        for i in range(own):
            gradient = jnp.where(lanes == i, gradient - RIDGE * weights[:, i : i + 1], gradient)
        gradient = gradient.astype(low)
        part = total(swap(gradient.reshape(nz, share, group), "z"))
        part = total(spread(part.astype(low), "y"))
        part = part.astype(low)
        if step > 0:
            places = step_places(step, steps, plane, own)
        part = side_by_side(spread(part, CELL))
        part = product(part, inverse, ((1,), (1,))).astype(low)
        part = product(part, places, ((1,), (1,))).astype(low)
        change = spread(part, "z").reshape(tall, group)[:high]
        update = product(change, kernel[block], ((1,), (0,))).astype(low)
        update = update.reshape(high, cell, own_rows).transpose(1, 0, 2)
        current = current - total(swap(update, CELL))
        if step < steps - 1:
            current_low = side_by_side(spread(current.astype(low), CELL))
        change_own = jnp.stack(
            [jnp.sum(jnp.where(lanes[:high] == i, change, 0.0), axis=1)[:classes] for i in range(own)]
        )
        results.append(block_weights[step] + change_own)
    return current[:classes].T, jnp.stack(results)


def solution(mesh):
    dp, blk = mesh.shape["dp"], mesh.shape["blk"]
    plane = dp // 2
    ny = 1 << (int(math.log2(plane)) // 2)
    fine = Mesh(mesh.devices.reshape(plane // ny, ny, 2, blk), ("z", "y", "c", "x"))
    placed = (
        P(DP, None),
        P((*DP, "x"), None),
        P(None, (*DP, "x"), None),
        P(None, None, (*DP, "x")),
        P(),
    )
    return jax.shard_map(
        on_device,
        mesh=fine,
        in_specs=placed,
        out_specs=(P((*DP, "x"), None), P(None, (*DP, "x"), None)),
        check_vma=False,
    )
```

```python
import math

import jax
import jax.numpy as jnp
from jax import lax
from jax.experimental import pallas as pl
from jax.experimental.pallas import tpu as pltpu
from jax.sharding import Mesh
from jax.sharding import PartitionSpec as P

RIDGE = 0.3
DP = ("z", "y", "c")
PLANE = ("z", "y")
CELL = ("c", "x")


def swap(pieces, axis):
    return lax.all_to_all(pieces, axis, 0, 0, tiled=True)


def spread(piece, axis):
    return swap(jnp.broadcast_to(piece[None], (lax.axis_size(axis), *piece.shape)), axis)


def ordered(piece, other, first):
    return jnp.stack([jnp.where(first, piece, other), jnp.where(first, other, piece)])


def total(pieces):
    return jnp.sum(pieces.astype(jnp.float32), axis=0)


def side_by_side(pieces):
    count, high, wide = pieces.shape
    return pieces.transpose(1, 0, 2).reshape(high, count * wide)


def product(left, right, dims, **options):
    return lax.dot_general(
        left, right, (dims, ((), ())), preferred_element_type=jnp.float32, **options
    )


def arranged(rows, numbers, plane, cell):
    steps, own, columns = rows.shape
    count, group = steps * own, plane * own
    if columns % 2048 or count != 8 or cell * own != 32:
        rows = rows.astype(jnp.bfloat16).reshape(count, plane, cell, own)
        numbers = numbers.reshape(steps, plane, cell, own).transpose(2, 0, 1, 3)
        return (
            rows.transpose(0, 2, 1, 3).reshape(count, columns),
            numbers.reshape(cell, steps, group),
        )
    blocks = columns // 128
    run = 128 // cell

    def kernel(rows_ref, numbers_ref, rows_out, numbers_out):
        number = numbers_ref[...]
        tall = [rows_ref[step] for step in range(steps)]
        tall += [(number >> 8).astype(jnp.float32), (number & 255).astype(jnp.float32)]
        tall += [jnp.zeros((16 - count - 2 * steps, columns), jnp.float32)]
        tall = jnp.concatenate(tall, axis=0)
        tall = jnp.concatenate([tall[:, 128 * q : 128 * (q + 1)] for q in range(blocks)], axis=0)
        source = lax.broadcasted_iota(jnp.int32, (128, 128), 0)
        target = lax.broadcasted_iota(jnp.int32, (128, 128), 1)
        member, lane = (source >> 2) & 7, ((source >> 5) << 2) | (source & 3)
        order = jnp.where(member * run + lane == target, 1.0, 0.0).astype(jnp.bfloat16)
        tall = jnp.dot(tall.astype(jnp.bfloat16), order, preferred_element_type=jnp.float32)
        part = lax.broadcasted_iota(jnp.int32, (16, 128), 1) >> 4
        wide = blocks // cell
        for out in range(blocks):
            member, first = out // wide, out % wide * cell
            joined = jnp.zeros((16, 128), jnp.float32)
            for k in range(cell):
                q = first + k
                piece = tall[16 * q : 16 * (q + 1)]
                if k != member:
                    piece = pltpu.roll(piece, (k - member) * run % 128, 1)
                joined = jnp.where(part == k, piece, joined)
            rows_out[:, 128 * out : 128 * (out + 1)] = joined[:count].astype(rows_out.dtype)
            number = joined[count : count + steps] * 256.0 + joined[count + steps : count + 2 * steps]
            at = out % wide * 128
            numbers_out[member, :, at : at + 128] = number.astype(jnp.int32)

    return pl.pallas_call(
        kernel,
        out_shape=(
            jax.ShapeDtypeStruct((count, columns), jnp.bfloat16),
            jax.ShapeDtypeStruct((cell, steps, group), jnp.int32),
        ),
        name="arrange",
    )(rows, numbers)


def step_places(step, steps, plane, own):
    shape = (plane * own, steps * plane * own)
    row = lax.broadcasted_iota(jnp.int32, shape, 0)
    source = row // own * (steps * own) + step * own + row % own
    return (source == lax.broadcasted_iota(jnp.int32, shape, 1)).astype(jnp.bfloat16)


def on_device(features, residual, block_weights, block_inverse, block_columns):
    nz, ny, nc, nx = (lax.axis_size(axis) for axis in ("z", "y", "c", "x"))
    plane, cell = nz * ny, nc * nx
    place, member = lax.axis_index(PLANE), lax.axis_index(CELL)
    width = features.shape[1]
    own_rows, classes = residual.shape
    steps, own, _ = block_weights.shape
    columns = block_columns.shape[1]
    group = plane * own
    high = -(-classes // 8) * 8
    share = -(-classes // (ny * 8)) * 8
    tall = ny * share
    gamma_rate = 4.0 / width
    low = jnp.bfloat16

    inverse, chosen = arranged(block_inverse.transpose(0, 2, 1), block_columns, plane, cell)
    inverse = lax.all_gather(inverse, PLANE, axis=0, tiled=True)
    current = jnp.pad(residual.T, ((0, high - classes), (0, 0)))
    first = lax.axis_index("c") == 0

    chosen = lax.dynamic_index_in_dim(chosen, member, 0, keepdims=False).reshape(steps * group)

    other = lax.ppermute(features, "c", [(0, 1), (1, 0)])
    frames = ordered(features, other, first).reshape(nc * features.shape[0], width)
    spots = lax.broadcasted_iota(jnp.int32, (steps * group, frames.shape[0]), 1)
    picks = ((chosen - place * frames.shape[0])[:, None] == spots).astype(low)
    part = product(picks, frames, ((1,), (0,))).astype(low)
    part, pair = lax.optimization_barrier((part, residual))
    pair = jnp.pad(pair.T, ((0, high - classes), (0, 0))).astype(low)
    pair = ordered(pair, lax.ppermute(pair, "c", [(0, 1), (1, 0)]), first)
    part = total(swap(part.reshape(plane, -1, width), PLANE)).astype(low)
    places = step_places(0, steps, plane, own)
    part, pair, places = lax.optimization_barrier((part, pair, places))
    pair = lax.all_gather(pair, "x")
    current_low = side_by_side(pair.swapaxes(0, 1).reshape(cell, high, own_rows))
    centers = spread(part, PLANE).reshape(steps * group, width)

    frame_f = frames.astype(jnp.float32)
    frame_sq = jnp.sum(frame_f * frame_f, axis=1)
    center_f = centers.astype(jnp.float32)
    center_sq = jnp.sum(center_f * center_f, axis=1)
    cross = product(centers, frames, ((1,), (1,)))
    kernel = jnp.exp(
        -gamma_rate * (frame_sq[None, :] + center_sq[:, None] - 2.0 * cross)
    ).astype(low)

    lanes = lax.broadcasted_iota(jnp.int32, (tall, group), 1) - place * own
    results = []
    for step in range(steps):
        block = slice(step * group, (step + 1) * group)
        weights = jnp.pad(block_weights[step].T, ((0, tall - classes), (0, 0)))
        current_low = jnp.pad(current_low, ((0, tall - high), (0, 0)))
        gradient = product(current_low, kernel[block], ((1,), (1,)))
        for i in range(own):
            gradient = jnp.where(lanes == i, gradient - RIDGE * weights[:, i : i + 1], gradient)
        gradient = gradient.astype(low)
        part = total(swap(gradient.reshape(ny, share, group), "y"))
        part = total(spread(part.astype(low), "z"))
        part = part.astype(low)
        if step > 0:
            places = step_places(step, steps, plane, own)
        part = side_by_side(spread(part, CELL))
        part = product(part, inverse, ((1,), (1,))).astype(low)
        part = product(part, places, ((1,), (1,))).astype(low)
        change = spread(part, "y").reshape(tall, group)[:high]
        update = product(change, kernel[block], ((1,), (0,))).astype(low)
        update = update.reshape(high, cell, own_rows).transpose(1, 0, 2)
        current = current - total(swap(update, CELL))
        if step < steps - 1:
            current_low = side_by_side(spread(current.astype(low), CELL))
        change_own = jnp.stack(
            [jnp.sum(jnp.where(lanes[:high] == i, change, 0.0), axis=1)[:classes] for i in range(own)]
        )
        results.append(block_weights[step] + change_own)
    return current[:classes].T, jnp.stack(results)


def solution(mesh):
    dp, blk = mesh.shape["dp"], mesh.shape["blk"]
    plane = dp // 2
    ny = 1 << (int(math.log2(plane)) // 2)
    fine = Mesh(mesh.devices.reshape(plane // ny, ny, 2, blk), ("z", "y", "c", "x"))
    placed = (
        P(DP, None),
        P((*DP, "x"), None),
        P(None, (*DP, "x"), None),
        P(None, None, (*DP, "x")),
        P(),
    )
    return jax.shard_map(
        on_device,
        mesh=fine,
        in_specs=placed,
        out_specs=(P((*DP, "x"), None), P(None, (*DP, "x"), None)),
        check_vma=False,
    )
```
